256 devices in a mesh: frame: 32 (over x, y, core), head: 8 (over z).
Axes of the slice: x: 4, y: 4, z: 8, core: 2. Of those that a mesh axis runs over, the one named last changes fastest.
Arguments:
- query_rows: bfloat16 [16384, 2048], P(('frame', 'head')), may hold values from -10 to 10
- key_rows: bfloat16 [16384, 2048], P(('frame', 'head')), may hold values from -10 to 10
- value_rows: bfloat16 [16384, 2048], P(('frame', 'head')), may hold values from -48 to 48
- out_grad: bfloat16 [16384, 2048], P(('frame', 'head')), may hold values from -48 to 48
- block_order: int32 [32, 4], replicated, may hold values from 0 to 3, each once within a row
Outputs:
- attended: bfloat16 [16384, 2048], P(('frame', 'head'))
- query_grad: bfloat16 [16384, 2048], P(('frame', 'head'))
- key_grad: bfloat16 [16384, 2048], P(('frame', 'head'))
- value_grad: bfloat16 [16384, 2048], P(('frame', 'head'))
The draws below stay inside these ranges and needn't reach their ends.
Inputs may be any that keep to these rules, and one draw needn't show every extreme that they name: `block_order`: each row holds every block index of a frame once.
All inputs are finite; a program needn't handle non-finite values.
Results may differ from the reference program's by a relative error of at most 0.028.
Values may be sent and summed in bfloat16 or wider, within the bound.
No kernel may reach another device: no remote copies, remote signals or barrier semaphores. Data moves between devices by JAX's collectives and lax.ppermute only.
A program may use at most 64 MiB of HBM per device.

```python
import math
import jax
import jax.numpy as jnp
from jax import lax

HD = 128
BLK = 128
BPF = 4
BANDS = 2
HEADS = 16
HID = 2048
TPF = 512
FRAMES = 32
TOKENS = 16384
KEYS = 1280


def drawn_pair(key):
    query_key = jax.random.fold_in(key, 11)
    other_key = jax.random.fold_in(key, 12)
    shape_all = (TOKENS, HEADS * HD)
    queries = jax.random.truncated_normal(query_key, -6.0, 6.0, shape_all, jnp.float32)
    keys_all = jax.random.truncated_normal(other_key, -6.0, 6.0, shape_all, jnp.float32)
    return (queries, keys_all)


def draw_query_rows(key, part):
    return drawn_pair(key)[0].astype(jnp.bfloat16)


def draw_key_rows(key, part):
    return drawn_pair(key)[1].astype(jnp.bfloat16)


def shard_levels(stream_key, extent, shards, low, largest):
    level = 1.0
    for dim, shards_of in shards:
        draws = jax.random.uniform(jax.random.fold_in(jax.random.fold_in(stream_key, 6), dim), (shards_of,), jnp.float32, low / len(shards), largest / len(shards))
        level = level * jnp.repeat(jnp.exp(draws), extent[dim] // shards_of).reshape((-1,) + (1,) * (len(extent) - 1 - dim))
    return level


def normal_values(rng, dims, deviation, reach, cuts=(), kind=jnp.bfloat16):
    result = jax.random.normal(rng, dims, jnp.float32) * deviation
    if len(cuts) > 0:
        result = shard_levels(rng, dims, cuts, -0.22, 0.18) * result
    return jnp.clip(result, min=-reach, max=reach).astype(kind)


def setup_inputs(seed: int = 0) -> dict:
    key_list = jax.random.split(jax.random.key(seed), 6)
    return {
        "query_rows": draw_query_rows(jax.random.fold_in(key_list[5], 71), 0),
        "key_rows": draw_key_rows(jax.random.fold_in(key_list[5], 71), 0),
        "value_rows": normal_values(key_list[2], (TOKENS, HID), 8.0, 48.0, ((0, 256),)),
        "out_grad": normal_values(key_list[3], (TOKENS, HID), 8.0, 48.0, ((0, 256),)),
        "block_order": jax.vmap(lambda own: jax.random.permutation(own, BPF))(jax.random.split(key_list[4], FRAMES)).reshape((FRAMES, BPF)).astype(jnp.int32),
    }


def frame_keys(block_order, frame_pos):
    token_range = jnp.arange(TPF, dtype=jnp.int32)
    block_range = jnp.arange(BLK, dtype=jnp.int32)
    index_parts = [frame_pos * TPF + token_range]
    valid_parts = [jnp.ones((TPF,), dtype=jnp.bool_)]
    for band_index in range(1, BANDS + 1):
        distance = 2 ** (band_index - 1)
        chosen_count = BPF >> band_index
        for partner in (frame_pos - distance, frame_pos + distance):
            inside = jnp.logical_and(partner >= 0, partner < FRAMES)
            clipped = jnp.clip(partner, 0, FRAMES - 1).astype(jnp.int32)
            order_row = lax.dynamic_slice(block_order, (clipped, jnp.int32(0)), (1, chosen_count))[0]
            token_rows = clipped * TPF + order_row[:, None] * BLK + block_range[None, :]
            index_parts.append(token_rows.reshape(-1).astype(jnp.int32))
            valid_parts.append(jnp.broadcast_to(inside, (chosen_count * BLK,)))
    return (jnp.concatenate(index_parts), jnp.concatenate(valid_parts))

def round_remote(part):
    remote = lax.optimization_barrier(part[TPF:].astype(jnp.bfloat16)).astype(jnp.float32)
    return jnp.concatenate([part[:TPF], remote], axis=0)

def reference(query_rows, key_rows, value_rows, out_grad, block_order):
    score_scale = 1.0 / math.sqrt(HD)
    width_all = HEADS * HD

    def one_frame(frame_index, loop_state):
        attended, query_grad, key_acc, value_acc = loop_state
        frame_pos = jnp.asarray(frame_index).astype(jnp.int32)
        key_index, key_valid = frame_keys(block_order, frame_pos)
        row_start = frame_pos * TPF
        query_here = lax.dynamic_slice_in_dim(query_rows, row_start, TPF, 0).astype(jnp.float32).reshape(TPF, HEADS, HD)
        grad_here = lax.dynamic_slice_in_dim(out_grad, row_start, TPF, 0).astype(jnp.float32).reshape(TPF, HEADS, HD)
        key_here = key_rows[key_index].astype(jnp.float32).reshape(KEYS, HEADS, HD)
        value_here = value_rows[key_index].astype(jnp.float32).reshape(KEYS, HEADS, HD)
        scores = jnp.einsum('qhd,khd->hqk', query_here, key_here) * score_scale
        scores = jnp.where(key_valid[None, None, :], scores, -jnp.inf)
        row_peak = lax.optimization_barrier(jnp.max(scores, axis=2, keepdims=True))
        row_total = lax.optimization_barrier(jnp.sum(jnp.exp(scores - row_peak), axis=2, keepdims=True))
        weights = jnp.exp(scores - (row_peak + jnp.log(row_total)))
        weights_low = lax.optimization_barrier(weights.astype(jnp.bfloat16)).astype(jnp.float32)
        out_frame = jnp.einsum('hqk,khd->qhd', weights_low, value_here).astype(jnp.bfloat16)
        out_wide = lax.optimization_barrier(out_frame).astype(jnp.float32)
        row_delta = lax.optimization_barrier(jnp.sum(grad_here * out_wide, axis=2))
        weight_grad = jnp.einsum('qhd,khd->hqk', grad_here, value_here)
        score_grad = (weights * (weight_grad - jnp.transpose(row_delta)[:, :, None])).astype(jnp.bfloat16)
        score_wide = lax.optimization_barrier(score_grad).astype(jnp.float32)
        query_part = (jnp.einsum('hqk,khd->qhd', score_wide, key_here) * score_scale).astype(jnp.bfloat16)
        key_part = jnp.einsum('hqk,qhd->khd', score_wide, query_here) * score_scale
        value_part = jnp.einsum('hqk,qhd->khd', weights_low, grad_here)
        key_part = round_remote(key_part)
        value_part = round_remote(value_part)
        attended = lax.dynamic_update_slice_in_dim(attended, out_frame.reshape(TPF, width_all), row_start, 0)
        query_grad = lax.dynamic_update_slice_in_dim(query_grad, query_part.reshape(TPF, width_all), row_start, 0)
        key_acc = key_acc.at[key_index].add(key_part.reshape(KEYS, width_all))
        value_acc = value_acc.at[key_index].add(value_part.reshape(KEYS, width_all))
        return (attended, query_grad, key_acc, value_acc)
    start_state = (jnp.zeros((TOKENS, width_all), jnp.bfloat16), jnp.zeros((TOKENS, width_all), jnp.bfloat16), jnp.zeros((TOKENS, width_all), jnp.float32), jnp.zeros((TOKENS, width_all), jnp.float32))
    attended, query_grad, key_acc, value_acc = lax.fori_loop(0, FRAMES, one_frame, start_state)
    return (attended, query_grad, key_acc.astype(jnp.bfloat16), value_acc.astype(jnp.bfloat16))
```

```python
import functools
import math

import jax
import jax.numpy as jnp
from jax import lax
from jax.experimental import pallas as pl
from jax.experimental.pallas import tpu as pltpu
from jax.sharding import PartitionSpec as P

HD = 128
BLK = 128
BF16 = jnp.bfloat16
F32 = jnp.float32
SCALE = 1.0 / math.sqrt(HD)
LOG2E = 1.0 / math.log(2.0)
VMEM_BYTES = 48 * 1024 * 1024

VM = pl.BlockSpec(memory_space=pltpu.VMEM)
SM = pl.BlockSpec(memory_space=pltpu.SMEM)


def call(body, out_shape, in_specs, out_specs, name):
    return pl.pallas_call(
        body,
        out_shape=out_shape,
        in_specs=in_specs,
        out_specs=out_specs,
        name=name,
        compiler_params=pltpu.CompilerParams(vmem_limit_bytes=VMEM_BYTES),
    )


def shifted(array, by):
    length = lax.axis_size("frame")
    pairs = [(i, i + by) for i in range(length) if 0 <= i + by < length]
    return lax.ppermute(array, "frame", pairs)


def pack_pair(first, second, parts):
    rows, width = first.shape
    piece = width // parts

    def body(a_ref, b_ref, out_ref):
        for part in range(parts):
            out_ref[part, 0] = a_ref[:, part * piece : (part + 1) * piece]
            out_ref[part, 1] = b_ref[:, part * piece : (part + 1) * piece]

    shape = jax.ShapeDtypeStruct((parts, 2, rows, piece), first.dtype)
    return call(body, shape, [VM, VM], VM, "pack_pair")(first, second)


def unpack_pair(packed):
    parts, _, rows, piece = packed.shape

    def body(in_ref, a_ref, b_ref):
        for part in range(parts):
            a_ref[:, part * piece : (part + 1) * piece] = in_ref[part, 0]
            b_ref[:, part * piece : (part + 1) * piece] = in_ref[part, 1]

    shape = jax.ShapeDtypeStruct((rows, parts * piece), packed.dtype)
    return call(body, [shape, shape], [VM], [VM, VM], "unpack_pair")(packed)


def pick_blocks(block_order, pair):
    _, _, rows, width = pair.shape
    per = BLK // rows

    def body(order_ref, pair_ref, near_ref, far_ref):
        frame = lax.axis_index("frame")
        for rank in range(2):
            start = order_ref[frame, rank] * per
            for i in range(per):
                taken = pair_ref[start + i]
                near_ref[rank * per + i] = taken
                if rank == 0:
                    far_ref[i] = taken

    near = jax.ShapeDtypeStruct((2 * per, 2, rows, width), pair.dtype)
    far = jax.ShapeDtypeStruct((per, 2, rows, width), pair.dtype)
    return call(body, [near, far], [SM, VM], [VM, VM], "pick_blocks")(block_order, pair)


def dot(a, b, contract):
    return lax.dot_general(a, b, ((contract[:1], contract[1:]), ((), ())), preferred_element_type=F32)


def attention_body(frame_count, pair_ref, query_ref, l1_ref, u1_ref, l2_ref, u2_ref,
                   first_ref, own_ref, gl1_ref, gu1_ref, gl2_ref, gu2_ref):
    frame = lax.axis_index("frame")
    parts, _, rows, width = pair_ref.shape
    tokens = parts * rows
    hidden = [None] + [
        jnp.where(seen, 0.0, -jnp.inf).astype(F32)
        for seen in (frame >= 1, frame + 1 < frame_count, frame >= 2, frame + 2 < frame_count)
    ]
    sources = (pair_ref, l1_ref, u1_ref, l2_ref, u2_ref)
    targets = (None, gl1_ref, gu1_ref, gl2_ref, gu2_ref)
    for head in range(width // HD):
        cols = slice(head * HD, (head + 1) * HD)
        query = query_ref[:, 0, :, cols].reshape(tokens, HD)
        grad = query_ref[:, 1, :, cols].reshape(tokens, HD)
        keys = [s[:, 0, :, cols].reshape(-1, HD) for s in sources]
        values = [s[:, 1, :, cols].reshape(-1, HD) for s in sources]
        scores = []
        for key, bias in zip(keys, hidden):
            part = dot(key, query, (1, 1)) * (SCALE * LOG2E)
            scores.append(part if bias is None else part + bias)
        peak = functools.reduce(jnp.maximum, [jnp.max(s, axis=0, keepdims=True) for s in scores])
        powers = [jnp.exp2(s - peak) for s in scores]
        total = functools.reduce(jnp.add, [jnp.sum(p, axis=0, keepdims=True) for p in powers])
        inverse = 1.0 / total
        weights = [p * inverse for p in powers]
        lows = [w.astype(BF16) for w in weights]
        out_t = functools.reduce(jnp.add, [dot(v, w, (0, 0)) for v, w in zip(values, lows)])
        out = out_t.astype(BF16)
        grad_t = grad.astype(F32).T
        delta = jnp.sum(grad_t * out.astype(F32), axis=0, keepdims=True)
        first_ref[:, 0, :, cols] = out_t.T.astype(BF16).reshape(parts, rows, HD)
        score_grads = [
            (w * (dot(v, grad, (1, 1)) - delta)).astype(BF16) for w, v in zip(weights, values)
        ]
        query_t = functools.reduce(jnp.add, [dot(k, d, (0, 0)) for k, d in zip(keys, score_grads)])
        first_ref[:, 1, :, cols] = (query_t * SCALE).T.astype(BF16).reshape(parts, rows, HD)
        for low, score_grad, target in zip(lows, score_grads, targets):
            key_part = dot(score_grad, query, (1, 0)) * SCALE
            value_part = dot(low, grad, (1, 0))
            if target is None:
                own_ref[:, 0, :, cols] = key_part.reshape(parts, rows, HD)
                own_ref[:, 1, :, cols] = value_part.reshape(parts, rows, HD)
            else:
                target[:, 0, :, cols] = key_part.astype(BF16).reshape(-1, rows, HD)
                target[:, 1, :, cols] = value_part.astype(BF16).reshape(-1, rows, HD)


def attention(pair, query, panels):
    shape = jax.ShapeDtypeStruct
    outs = [shape(pair.shape, BF16), shape(pair.shape, F32)] + [shape(p.shape, BF16) for p in panels]
    body = functools.partial(attention_body, lax.axis_size("frame"))
    return call(body, outs, [VM] * 6, [VM] * 6, "attention")(pair, query, *panels)


def add_returned(block_order, own, returned):
    parts, _, rows, width = own.shape
    per = BLK // rows

    def body(order_ref, own_ref, a1_ref, b1_ref, a2_ref, b2_ref, out_ref):
        frame = lax.axis_index("frame")
        out_ref[...] = own_ref[...].astype(BF16)
        for rank in range(2):
            start = order_ref[frame, rank] * per
            for i in range(per):
                at = rank * per + i
                term = a1_ref[at].astype(F32) + b1_ref[at].astype(F32)
                if rank == 0:
                    term = term + (a2_ref[i].astype(F32) + b2_ref[i].astype(F32))
                out_ref[start + i] = (own_ref[start + i] + term).astype(BF16)

    return call(
        body, jax.ShapeDtypeStruct(own.shape, BF16), [SM] + [VM] * 5, VM, "add_returned"
    )(block_order, own, *returned)


def exchange(packed):
    return lax.all_to_all(packed, "head", 0, 0)


def local(query_rows, key_rows, value_rows, out_grad, block_order):
    parts = lax.axis_size("head")
    pair = exchange(pack_pair(key_rows, value_rows, parts))
    query = exchange(pack_pair(query_rows, out_grad, parts))
    near, far = pick_blocks(block_order, pair)
    panels = (shifted(near, 1), shifted(near, -1), shifted(far, 2), shifted(far, -2))
    first, own, low1, up1, low2, up2 = attention(pair, query, panels)
    returned = (shifted(low1, -1), shifted(up1, 1), shifted(low2, -2), shifted(up2, 2))
    attended, query_grad = unpack_pair(exchange(first))
    second = add_returned(block_order, own, returned)
    key_grad, value_grad = unpack_pair(exchange(second))
    return (attended, query_grad, key_grad, value_grad)


def solution(mesh):
    rows = P(("frame", "head"), None)
    return jax.shard_map(
        local,
        mesh=mesh,
        in_specs=(rows, rows, rows, rows, P()),
        out_specs=(rows, rows, rows, rows),
        check_vma=False,
    )
```

```python
import functools
import math

import jax
import jax.numpy as jnp
from jax import lax
from jax.experimental import pallas as pl
from jax.experimental.pallas import tpu as pltpu
from jax.sharding import PartitionSpec as P

HD = 128
BLK = 128
BF16 = jnp.bfloat16
F32 = jnp.float32
SCALE = 1.0 / math.sqrt(HD)
LOG2E = 1.0 / math.log(2.0)
MIB = 1024 * 1024
MASKS = (0, 1, 7, 3, 2, 6, 5, 4)

VM = pl.BlockSpec(memory_space=pltpu.VMEM)
SM = pl.BlockSpec(memory_space=pltpu.SMEM)


def call(body, out_shape, in_specs, out_specs, name, mib, scratch_shapes=()):
    return pl.pallas_call(
        body,
        out_shape=out_shape,
        in_specs=in_specs,
        out_specs=out_specs,
        scratch_shapes=scratch_shapes,
        name=name,
        compiler_params=pltpu.CompilerParams(vmem_limit_bytes=mib * MIB),
    )


def swapped(array, distance, start):
    length = lax.axis_size("frame")
    pairs = []
    for first in range(start, length, 2 * distance):
        for low in range(first, min(first + distance, length - distance)):
            pairs += [(low, low + distance), (low + distance, low)]
    return lax.ppermute(array, "frame", pairs)


SWAPS = ((1, 0), (1, 1), (2, 0), (2, 2))


def has_partner(frame, length, distance, start):
    shifted = frame + (2 * distance - start)
    lower_half = lax.rem(shifted, 2 * distance) < distance
    partner = jnp.where(lower_half, frame + distance, frame - distance)
    return jnp.logical_and(jnp.logical_and(partner >= 0, partner < length), frame >= 0)


def head_swaps(pieces):
    length = lax.axis_size("head")
    return [
        lax.ppermute(piece, "head", [(i, i ^ mask) for i in range(length)]) if mask else piece
        for piece, mask in zip(pieces, MASKS)
    ]


def place_of(slot):
    return jnp.bitwise_xor(lax.axis_index("head"), MASKS[slot])


def columns_of(slot, piece):
    return pl.ds(pl.multiple_of(place_of(slot) * piece, piece), piece)


def pack(arrays, parts):
    rows, width = arrays[0].shape
    count = len(arrays)
    piece = width // parts

    def body(*refs):
        in_refs, out_refs, sem = refs[:count], refs[count:-1], refs[-1]
        copies = []
        for k, out_ref in enumerate(out_refs):
            for i, ref in enumerate(in_refs):
                copies.append(
                    pltpu.make_async_copy(ref.at[:, columns_of(k, piece)], out_ref.at[i], sem.at[k, i])
                )
        for copy in copies:
            copy.start()
        for copy in copies:
            copy.wait()

    shape = jax.ShapeDtypeStruct((count, rows, piece), arrays[0].dtype)
    anywhere = pl.BlockSpec(memory_space=pltpu.HBM)
    arrays = [pltpu.with_memory_space_constraint(array, pltpu.HBM) for array in arrays]
    sems = [pltpu.SemaphoreType.DMA((parts, count))]
    return call(body, [shape] * parts, [anywhere] * count, [VM] * parts, "pack", 4, sems)(*arrays)


def unpack(pieces):
    parts = len(pieces)
    count, rows, piece = pieces[0].shape

    def body(*refs):
        for i, ref in enumerate(refs[parts:]):
            for k in range(parts):
                ref[:, columns_of(k, piece)] = refs[k][i]

    shape = jax.ShapeDtypeStruct((rows, parts * piece), pieces[0].dtype)
    return call(body, [shape] * count, [VM] * parts, [VM] * count, "unpack", 8)(*pieces)


def pick_blocks(block_order, pieces):
    parts = len(pieces)
    _, rows, width = pieces[0].shape
    per = BLK // rows

    def body(order_ref, *refs):
        near_ref, far_ref, all_ref = refs[parts:]
        frame = lax.axis_index("frame")
        for k in range(parts):
            all_ref[place_of(k)] = refs[k][0:2]
        for rank in range(2):
            start = order_ref[rank, frame] * per
            for i in range(per):
                taken = all_ref[start + i]
                near_ref[rank * per + i] = taken
                if rank == 0:
                    far_ref[i] = taken

    near = jax.ShapeDtypeStruct((2 * per, 2, rows, width), BF16)
    far = jax.ShapeDtypeStruct((per, 2, rows, width), BF16)
    scratch = [pltpu.VMEM((parts, 2, rows, width), BF16)]
    return call(
        body, [near, far], [SM] + [VM] * parts, [VM, VM], "pick_blocks", 8, scratch
    )(block_order.T, *pieces)


def dot(a, b, contract):
    return lax.dot_general(a, b, ((contract[:1], contract[1:]), ((), ())), preferred_element_type=F32)


def attention_body(frame_count, parts, *refs):
    piece_refs, panel_refs = refs[:parts], refs[parts : parts + 4]
    first_ref, own_ref, *targets = refs[parts + 4 :]
    frame = lax.axis_index("frame")
    _, rows, width = piece_refs[0].shape
    hidden = [None] + [
        jnp.where(has_partner(frame, frame_count, *swap), 0.0, -jnp.inf).astype(F32) for swap in SWAPS
    ]
    for head in range(width // HD):
        cols = slice(head * HD, (head + 1) * HD)
        key, value, query, grad = [
            jnp.concatenate([ref[i, :, cols] for ref in piece_refs], axis=0) for i in range(4)
        ]
        keys = [key] + [ref[:, 0, :, cols].reshape(-1, HD) for ref in panel_refs]
        values = [value] + [ref[:, 1, :, cols].reshape(-1, HD) for ref in panel_refs]
        scores = []
        for key, bias in zip(keys, hidden):
            part = dot(key, query, (1, 1)) * (SCALE * LOG2E)
            scores.append(part if bias is None else part + bias)
        peak = functools.reduce(jnp.maximum, [jnp.max(s, axis=0, keepdims=True) for s in scores])
        powers = [jnp.exp2(s - peak) for s in scores]
        total = functools.reduce(jnp.add, [jnp.sum(p, axis=0, keepdims=True) for p in powers])
        inverse = 1.0 / total
        weights = [p * inverse for p in powers]
        lows = [w.astype(BF16) for w in weights]
        out_t = functools.reduce(jnp.add, [dot(v, w, (0, 0)) for v, w in zip(values, lows)])
        out = out_t.astype(BF16)
        grad_t = grad.astype(F32).T
        delta = jnp.sum(grad_t * out.astype(F32), axis=0, keepdims=True)
        first_ref[:, 0, :, cols] = out_t.T.astype(BF16).reshape(parts, rows, HD)
        score_grads = [
            (w * (dot(v, grad, (1, 1)) - delta)).astype(BF16) for w, v in zip(weights, values)
        ]
        query_t = functools.reduce(jnp.add, [dot(k, d, (0, 0)) for k, d in zip(keys, score_grads)])
        first_ref[:, 1, :, cols] = (query_t * SCALE).T.astype(BF16).reshape(parts, rows, HD)
        for low, score_grad, target in zip(lows, score_grads, [None] + targets):
            key_part = dot(score_grad, query, (1, 0)) * SCALE
            value_part = dot(low, grad, (1, 0))
            if target is None:
                own_ref[:, 0, :, cols] = key_part.reshape(parts, rows, HD)
                own_ref[:, 1, :, cols] = value_part.reshape(parts, rows, HD)
            else:
                target[:, 0, :, cols] = key_part.astype(BF16).reshape(-1, rows, HD)
                target[:, 1, :, cols] = value_part.astype(BF16).reshape(-1, rows, HD)


def attention(pieces, panels):
    parts = len(pieces)
    _, rows, width = pieces[0].shape
    shape = jax.ShapeDtypeStruct
    two = (parts, 2, rows, width)
    outs = [shape(two, BF16), shape(two, F32)] + [shape(p.shape, BF16) for p in panels]
    body = functools.partial(attention_body, lax.axis_size("frame"), parts)
    return call(body, outs, [VM] * (parts + 4), [VM] * 6, "attention", 32)(*pieces, *panels)


def add_returned(block_order, first, own, returned):
    parts, _, rows, width = own.shape
    per = BLK // rows

    def body(order_ref, first_ref, own_ref, a1_ref, b1_ref, a2_ref, b2_ref, *refs):
        out_refs, sum_ref = refs[:parts], refs[parts]
        frame = lax.axis_index("frame")
        for k in range(parts):
            sum_ref[place_of(k)] = own_ref[k]
        for rank in range(2):
            start = order_ref[rank, frame] * per
            for i in range(per):
                at = rank * per + i
                term = a1_ref[at].astype(F32) + b1_ref[at].astype(F32)
                if rank == 0:
                    term = term + (a2_ref[i].astype(F32) + b2_ref[i].astype(F32))
                sum_ref[start + i] = sum_ref[start + i] + term
        for k in range(parts):
            out_refs[k][0:2] = sum_ref[place_of(k)].astype(BF16)
            out_refs[k][2:4] = first_ref[k]

    shape = jax.ShapeDtypeStruct((4, rows, width), BF16)
    scratch = [pltpu.VMEM(own.shape, F32)]
    return call(
        body, [shape] * parts, [SM] + [VM] * 6, [VM] * parts, "add_returned", 10, scratch
    )(block_order.T, first, own, *returned)


def local(query_rows, key_rows, value_rows, out_grad, block_order):
    parts = lax.axis_size("head")
    arrived = head_swaps(pack((key_rows, value_rows, query_rows, out_grad), parts))
    near, far = pick_blocks(block_order, arrived)
    panels = [swapped(far if swap[0] == 2 else near, *swap) for swap in SWAPS]
    first, own, *parts_of_others = attention(arrived, panels)
    returned = [swapped(part, *swap) for part, swap in zip(parts_of_others, SWAPS)]
    leaving = add_returned(block_order, first, own, returned)
    key_grad, value_grad, attended, query_grad = unpack(head_swaps(leaving))
    return (attended, query_grad, key_grad, value_grad)


def solution(mesh):
    rows = P(("frame", "head"), None)
    return jax.shard_map(
        local,
        mesh=mesh,
        in_specs=(rows, rows, rows, rows, P()),
        out_specs=(rows, rows, rows, rows),
        check_vma=False,
    )
```

```python
import functools
import math

import jax
import jax.numpy as jnp
from jax import lax
from jax.experimental import pallas as pl
from jax.experimental.pallas import tpu as pltpu
from jax.sharding import PartitionSpec as P

HD = 128
BLK = 128
BF16 = jnp.bfloat16
F32 = jnp.float32
SCALE = 1.0 / math.sqrt(HD)
LOG2E = 1.0 / math.log(2.0)
MIB = 1024 * 1024
SHIFTS = (0, 1, 7, 2, 6, 3, 5, 4)

VM = pl.BlockSpec(memory_space=pltpu.VMEM)
SM = pl.BlockSpec(memory_space=pltpu.SMEM)


def call(body, out_shape, in_specs, out_specs, name, mib, scratch_shapes=()):
    return pl.pallas_call(
        body,
        out_shape=out_shape,
        in_specs=in_specs,
        out_specs=out_specs,
        scratch_shapes=scratch_shapes,
        name=name,
        compiler_params=pltpu.CompilerParams(vmem_limit_bytes=mib * MIB),
    )


def swapped(array, distance, start):
    length = lax.axis_size("frame")
    pairs = []
    for first in range(start, length, 2 * distance):
        for low in range(first, min(first + distance, length - distance)):
            pairs += [(low, low + distance), (low + distance, low)]
    return lax.ppermute(array, "frame", pairs)


SWAPS = ((1, 0), (1, 1), (2, 0), (2, 2))


def has_partner(frame, length, distance, start):
    shifted = frame + (2 * distance - start)
    lower_half = lax.rem(shifted, 2 * distance) < distance
    partner = jnp.where(lower_half, frame + distance, frame - distance)
    return jnp.logical_and(jnp.logical_and(partner >= 0, partner < length), frame >= 0)


def head_shifts(pieces, sign):
    length = lax.axis_size("head")
    arrived = []
    for piece, by in zip(pieces, SHIFTS):
        if by:
            flat = piece.reshape(-1, piece.shape[-1])
            flat = lax.ppermute(flat, "head", [(i, (i + sign * by) % length) for i in range(length)])
            piece = flat.reshape(piece.shape)
        arrived.append(piece)
    return arrived


def place_above(slot):
    length = lax.axis_size("head")
    return lax.rem(lax.axis_index("head") + SHIFTS[slot], length)


def place_below(slot):
    length = lax.axis_size("head")
    return lax.rem(lax.axis_index("head") + (length - SHIFTS[slot]), length)


def columns_of(slot, piece):
    return pl.ds(pl.multiple_of(place_above(slot) * piece, piece), piece)


def pack(arrays, parts):
    rows, width = arrays[0].shape
    count = len(arrays)
    piece = width // parts

    def body(*refs):
        in_refs, out_refs, sem = refs[:count], refs[count:-1], refs[-1]
        copies = []
        for k, out_ref in enumerate(out_refs):
            for i, ref in enumerate(in_refs):
                copies.append(
                    pltpu.make_async_copy(ref.at[:, columns_of(k, piece)], out_ref.at[i], sem.at[k, i])
                )
        for copy in copies:
            copy.start()
        for copy in copies:
            copy.wait()

    shape = jax.ShapeDtypeStruct((count, rows, piece), arrays[0].dtype)
    anywhere = pl.BlockSpec(memory_space=pltpu.HBM)
    arrays = [pltpu.with_memory_space_constraint(array, pltpu.HBM) for array in arrays]
    sems = [pltpu.SemaphoreType.DMA((parts, count))]
    return call(body, [shape] * parts, [anywhere] * count, [VM] * parts, "pack", 4, sems)(*arrays)


def unpack(pieces):
    parts = len(pieces)
    count, rows, piece = pieces[0].shape

    def body(*refs):
        for i, ref in enumerate(refs[parts:]):
            for k in range(parts):
                ref[:, columns_of(k, piece)] = refs[k][i]

    shape = jax.ShapeDtypeStruct((rows, parts * piece), pieces[0].dtype)
    return call(body, [shape] * count, [VM] * parts, [VM] * count, "unpack", 8)(*pieces)


def pick_blocks(block_order, pieces):
    parts = len(pieces)
    _, rows, width = pieces[0].shape
    per = BLK // rows

    def body(order_ref, *refs):
        near_ref, far_ref, all_ref = refs[parts:]
        frame = lax.axis_index("frame")
        for k in range(parts):
            all_ref[place_below(k)] = refs[k][0:2]
        for rank in range(2):
            start = order_ref[rank, frame] * per
            for i in range(per):
                taken = all_ref[start + i]
                near_ref[rank * per + i] = taken
                if rank == 0:
                    far_ref[i] = taken

    near = jax.ShapeDtypeStruct((2 * per, 2, rows, width), BF16)
    far = jax.ShapeDtypeStruct((per, 2, rows, width), BF16)
    scratch = [pltpu.VMEM((parts, 2, rows, width), BF16)]
    return call(
        body, [near, far], [SM] + [VM] * parts, [VM, VM], "pick_blocks", 8, scratch
    )(block_order, *pieces)


def dot(a, b, contract):
    return lax.dot_general(a, b, ((contract[:1], contract[1:]), ((), ())), preferred_element_type=F32)


def columns(head):
    return slice(head * HD, (head + 1) * HD)


def rows_of(refs, i, head):
    return jnp.concatenate([ref[i, :, columns(head)] for ref in refs], axis=0)


def own_scores_body(*refs):
    piece_refs, (power_ref, weight_grad_ref, stats_ref) = refs[:-3], refs[-3:]
    for head in range(piece_refs[0].shape[-1] // HD):
        key, value, query, grad = [rows_of(piece_refs, i, head) for i in range(4)]
        scores = dot(key, query, (1, 1)) * (SCALE * LOG2E)
        weight_grad = dot(value, grad, (1, 1))
        peak = jnp.max(scores, axis=0, keepdims=True)
        power = jnp.exp2(scores - peak)
        power_ref[head] = power
        weight_grad_ref[head] = weight_grad
        stats_ref[head, 0:1] = peak
        stats_ref[head, 1:2] = jnp.sum(power, axis=0, keepdims=True)
        stats_ref[head, 2:3] = jnp.sum(power * weight_grad, axis=0, keepdims=True)


def own_scores(pieces):
    tokens = len(pieces) * pieces[0].shape[1]
    heads = pieces[0].shape[-1] // HD
    square = jax.ShapeDtypeStruct((heads, tokens, tokens), F32)
    stats = jax.ShapeDtypeStruct((heads, 8, tokens), F32)
    return call(
        own_scores_body, [square, square, stats], [VM] * len(pieces), [VM] * 3, "own_scores", 16
    )(*pieces)


def remote_part_body(frame_count, parts, *refs):
    piece_refs, panel_refs, stats_ref = refs[:parts], refs[parts : parts + 4], refs[parts + 4]
    joint_ref, *rest = refs[parts + 5 :]
    target_refs, low_refs, score_grad_refs = rest[:4], rest[4:8], rest[8:]
    frame = lax.axis_index("frame")
    rows = piece_refs[0].shape[1]
    heads = range(piece_refs[0].shape[-1] // HD)
    hidden = [
        jnp.where(has_partner(frame, frame_count, *swap), 0.0, -jnp.inf).astype(F32) for swap in SWAPS
    ]
    queries = [rows_of(piece_refs, 2, head) for head in heads]
    grads = [rows_of(piece_refs, 3, head) for head in heads]
    scores = [
        [
            dot(ref[:, 0, :, columns(head)].reshape(-1, HD), queries[head], (1, 1)) * (SCALE * LOG2E) + bias
            for ref, bias in zip(panel_refs, hidden)
        ]
        for head in heads
    ]
    weight_grads = [
        [dot(ref[:, 1, :, columns(head)].reshape(-1, HD), grads[head], (1, 1)) for ref in panel_refs]
        for head in heads
    ]
    for head in heads:
        own_peak = stats_ref[head, 0:1]
        peaks = [jnp.max(s, axis=0, keepdims=True) for s in scores[head]]
        peak = functools.reduce(jnp.maximum, peaks, own_peak)
        powers = [jnp.exp2(s - peak) for s in scores[head]]
        rescale = jnp.exp2(own_peak - peak)
        total = functools.reduce(
            jnp.add, [jnp.sum(p, axis=0, keepdims=True) for p in powers], stats_ref[head, 1:2] * rescale
        )
        moment = functools.reduce(
            jnp.add,
            [jnp.sum(p * g, axis=0, keepdims=True) for p, g in zip(powers, weight_grads[head])],
            stats_ref[head, 2:3] * rescale,
        )
        inverse = 1.0 / total
        delta = moment * inverse
        joint_ref[head, 0:1] = rescale * inverse
        joint_ref[head, 1:2] = delta
        for power, weight_grad, low_ref, score_grad_ref in zip(
            powers, weight_grads[head], low_refs, score_grad_refs
        ):
            weights = power * inverse
            low_ref[head] = weights.astype(BF16)
            score_grad_ref[head] = (weights * (weight_grad - delta)).astype(BF16)
    for head in heads:
        cols = columns(head)
        for target, low_ref, score_grad_ref in zip(target_refs, low_refs, score_grad_refs):
            key_part = dot(score_grad_ref[head], queries[head], (1, 0)) * SCALE
            value_part = dot(low_ref[head], grads[head], (1, 0))
            target[:, 0, :, cols] = key_part.astype(BF16).reshape(-1, rows, HD)
            target[:, 1, :, cols] = value_part.astype(BF16).reshape(-1, rows, HD)


def remote_part(pieces, panels, stats):
    parts = len(pieces)
    _, rows, width = pieces[0].shape
    shape = jax.ShapeDtypeStruct
    squares = [shape((width // HD, p.shape[0] * rows, parts * rows), BF16) for p in panels]
    outs = [shape(stats.shape, F32)] + [shape(p.shape, BF16) for p in panels] + squares + squares
    body = functools.partial(remote_part_body, lax.axis_size("frame"), parts)
    outs = call(body, outs, [VM] * (parts + 5), [VM] * 13, "remote_part", 24)(*pieces, *panels, stats)
    return outs[0], outs[1:5], outs[5:9], outs[9:]


def own_grads_body(parts, *refs):
    piece_refs, panel_refs, refs = refs[:parts], refs[parts : parts + 4], refs[parts + 4 :]
    power_ref, weight_grad_ref, joint_ref = refs[:3]
    low_refs, score_grad_refs, (first_ref, own_ref) = refs[3:7], refs[7:11], refs[11:]
    _, rows, width = piece_refs[0].shape
    for head in range(width // HD):
        cols = columns(head)
        key, value, query, grad = [rows_of(piece_refs, i, head) for i in range(4)]
        weights = power_ref[head] * joint_ref[head, 0:1]
        score_grad = (weights * (weight_grad_ref[head] - joint_ref[head, 1:2])).astype(BF16)
        low = weights.astype(BF16)
        own_ref[:, 0, :, cols] = (dot(score_grad, query, (1, 0)) * SCALE).reshape(parts, rows, HD)
        own_ref[:, 1, :, cols] = dot(low, grad, (1, 0)).reshape(parts, rows, HD)
        query_t = dot(key, score_grad, (0, 0))
        out_t = dot(value, low, (0, 0))
        for panel_ref, low_ref, score_grad_ref in zip(panel_refs, low_refs, score_grad_refs):
            query_t = query_t + dot(panel_ref[:, 0, :, cols].reshape(-1, HD), score_grad_ref[head], (0, 0))
            out_t = out_t + dot(panel_ref[:, 1, :, cols].reshape(-1, HD), low_ref[head], (0, 0))
        attended = out_t.T.astype(BF16)
        query_grad = (query_t * SCALE).T.astype(BF16)
        for slot in range(parts):
            first_ref[slot, 0, :, cols] = attended[slot * rows : (slot + 1) * rows]
            first_ref[slot, 1, :, cols] = query_grad[slot * rows : (slot + 1) * rows]


def own_grads(pieces, panels, power, weight_grad, joint, lows, score_grads):
    parts = len(pieces)
    _, rows, width = pieces[0].shape
    two = (parts, 2, rows, width)
    outs = [jax.ShapeDtypeStruct(two, BF16), jax.ShapeDtypeStruct(two, F32)]
    body = functools.partial(own_grads_body, parts)
    return call(body, outs, [VM] * (parts + 15), [VM] * 2, "own_grads", 16)(
        *pieces, *panels, power, weight_grad, joint, *lows, *score_grads
    )


def add_returned(block_order, first, own, returned):
    parts, _, rows, width = own.shape
    per = BLK // rows

    def body(order_ref, first_ref, own_ref, a1_ref, b1_ref, a2_ref, b2_ref, *refs):
        out_refs, sum_ref = refs[:parts], refs[parts]
        frame = lax.axis_index("frame")
        for k in range(parts):
            sum_ref[place_below(k)] = own_ref[k]
        for rank in range(2):
            start = order_ref[rank, frame] * per
            for i in range(per):
                at = rank * per + i
                term = a1_ref[at].astype(F32) + b1_ref[at].astype(F32)
                if rank == 0:
                    term = term + (a2_ref[i].astype(F32) + b2_ref[i].astype(F32))
                sum_ref[start + i] = sum_ref[start + i] + term
        for k in range(parts):
            out_refs[k][0:2] = sum_ref[place_below(k)].astype(BF16)
            out_refs[k][2:4] = first_ref[k]

    shape = jax.ShapeDtypeStruct((4, rows, width), BF16)
    scratch = [pltpu.VMEM(own.shape, F32)]
    return call(
        body, [shape] * parts, [SM] + [VM] * 6, [VM] * parts, "add_returned", 10, scratch
    )(block_order, first, own, *returned)


def local(query_rows, key_rows, value_rows, out_grad, block_order):
    parts = lax.axis_size("head")
    block_order = pltpu.with_memory_space_constraint(block_order.T, pltpu.HBM)
    arrived = head_shifts(pack((key_rows, value_rows, query_rows, out_grad), parts), 1)
    near, far = pick_blocks(block_order, arrived)
    panels = [swapped(far if swap[0] == 2 else near, *swap) for swap in SWAPS]
    power, weight_grad, stats = own_scores(arrived)
    joint, parts_of_others, lows, score_grads = remote_part(arrived, panels, stats)
    returned = [swapped(part, *swap) for part, swap in zip(parts_of_others, SWAPS)]
    first, own = own_grads(arrived, panels, power, weight_grad, joint, lows, score_grads)
    leaving = add_returned(block_order, first, own, returned)
    key_grad, value_grad, attended, query_grad = unpack(head_shifts(leaving, -1))
    return (attended, query_grad, key_grad, value_grad)


def solution(mesh):
    rows = P(("frame", "head"), None)
    return jax.shard_map(
        local,
        mesh=mesh,
        in_specs=(rows, rows, rows, rows, P()),
        out_specs=(rows, rows, rows, rows),
        check_vma=False,
    )
```

```python
import functools
import math

import jax
import jax.numpy as jnp
from jax import lax
from jax.experimental import pallas as pl
from jax.experimental.pallas import tpu as pltpu
from jax.sharding import PartitionSpec as P

HD = 128
BLK = 128
BF16 = jnp.bfloat16
F32 = jnp.float32
SCALE = 1.0 / math.sqrt(HD)
LOG2E = 1.0 / math.log(2.0)
MIB = 1024 * 1024
SHIFTS = (0, 1, 7, 2, 6, 3, 5, 4)

LOWEST = -1e30

VM = pl.BlockSpec(memory_space=pltpu.VMEM)
SM = pl.BlockSpec(memory_space=pltpu.SMEM)


def call(body, out_shape, in_specs, out_specs, name, mib, scratch_shapes=()):
    return pl.pallas_call(
        body,
        out_shape=out_shape,
        in_specs=in_specs,
        out_specs=out_specs,
        scratch_shapes=scratch_shapes,
        name=name,
        compiler_params=pltpu.CompilerParams(vmem_limit_bytes=mib * MIB),
    )


def swapped(array, distance, start):
    length = lax.axis_size("frame")
    pairs = []
    for first in range(start, length, 2 * distance):
        for low in range(first, min(first + distance, length - distance)):
            pairs += [(low, low + distance), (low + distance, low)]
    return lax.ppermute(array, "frame", pairs)


SWAPS = ((1, 0), (1, 1), (2, 0), (2, 2))


def has_partner(frame, length, distance, start):
    shifted = frame + (2 * distance - start)
    lower_half = lax.rem(shifted, 2 * distance) < distance
    partner = jnp.where(lower_half, frame + distance, frame - distance)
    return jnp.logical_and(jnp.logical_and(partner >= 0, partner < length), frame >= 0)


def head_shifts(pieces, sign):
    frames, length = lax.axis_size("frame"), lax.axis_size("head")
    arrived = []
    for piece, by in zip(pieces, SHIFTS):
        if by:
            pairs = []
            for frame in range(frames):
                step = -sign * by if frame % 2 else sign * by
                pairs += [(frame * length + i, frame * length + (i + step) % length) for i in range(length)]
            flat = piece.reshape(-1, piece.shape[-1])
            piece = lax.ppermute(flat, ("frame", "head"), pairs).reshape(piece.shape)
        arrived.append(piece)
    return arrived


def moved(step):
    length = lax.axis_size("head")
    odd = lax.rem(lax.axis_index("frame"), 2)
    return lax.rem(lax.axis_index("head") + length + step * (1 - 2 * odd), length)


def place_above(slot):
    return moved(SHIFTS[slot])


def place_below(slot):
    return moved(-SHIFTS[slot])


def columns_of(slot, piece):
    return pl.ds(pl.multiple_of(place_above(slot) * piece, piece), piece)


def pack(arrays, parts):
    rows, width = arrays[0].shape
    count = len(arrays)
    piece = width // parts

    def body(*refs):
        in_refs, out_refs, sem = refs[:count], refs[count:-1], refs[-1]
        copies = []
        for k, out_ref in enumerate(out_refs):
            for i, ref in enumerate(in_refs):
                copies.append(
                    pltpu.make_async_copy(ref.at[:, columns_of(k, piece)], out_ref.at[i], sem.at[k, i])
                )
        for copy in copies:
            copy.start()
        for copy in copies:
            copy.wait()

    shape = jax.ShapeDtypeStruct((count, rows, piece), arrays[0].dtype)
    anywhere = pl.BlockSpec(memory_space=pltpu.HBM)
    arrays = [pltpu.with_memory_space_constraint(array, pltpu.HBM) for array in arrays]
    sems = [pltpu.SemaphoreType.DMA((parts, count))]
    return call(body, [shape] * parts, [anywhere] * count, [VM] * parts, "pack", 4, sems)(*arrays)


def unpack(pieces):
    parts = len(pieces)
    count, rows, piece = pieces[0].shape

    def body(*refs):
        for i, ref in enumerate(refs[parts:]):
            for k in range(parts):
                ref[:, columns_of(k, piece)] = refs[k][i]

    shape = jax.ShapeDtypeStruct((rows, parts * piece), pieces[0].dtype)
    return call(body, [shape] * count, [VM] * parts, [VM] * count, "unpack", 8)(*pieces)


def pick_blocks(block_order, pieces):
    parts = len(pieces)
    _, rows, width = pieces[0].shape
    per = BLK // rows

    def body(order_ref, *refs):
        near_ref, far_ref, all_ref = refs[parts:]
        frame = lax.axis_index("frame")
        for k in range(parts):
            all_ref[place_below(k)] = refs[k][0:2]
        for rank in range(2):
            start = order_ref[rank, frame] * per
            for i in range(per):
                taken = all_ref[start + i]
                near_ref[rank * per + i] = taken
                if rank == 0:
                    far_ref[i] = taken

    near = jax.ShapeDtypeStruct((2 * per, 2, rows, width), BF16)
    far = jax.ShapeDtypeStruct((per, 2, rows, width), BF16)
    scratch = [pltpu.VMEM((parts, 2, rows, width), BF16)]
    return call(
        body, [near, far], [SM] + [VM] * parts, [VM, VM], "pick_blocks", 8, scratch
    )(block_order, *pieces)


def dot(a, b, contract):
    return lax.dot_general(a, b, ((contract[:1], contract[1:]), ((), ())), preferred_element_type=F32)


def columns(head):
    return slice(head * HD, (head + 1) * HD)


def rows_of(refs, i, head):
    return jnp.concatenate([ref[i, :, columns(head)] for ref in refs], axis=0)


def panel_rows(refs, i, head):
    return jnp.concatenate([ref[:, i, :, columns(head)].reshape(-1, HD) for ref in refs], axis=0)


def own_scores_body(*refs):
    piece_refs, (power_ref, weight_grad_ref, stats_ref) = refs[:-3], refs[-3:]
    for head in range(piece_refs[0].shape[-1] // HD):
        key, value, query, grad = [rows_of(piece_refs, i, head) for i in range(4)]
        scores = dot(key, query, (1, 1))
        weight_grad = dot(value, grad, (1, 1))
        peak = jnp.max(scores, axis=0, keepdims=True)
        power = jnp.exp2((scores - peak) * (SCALE * LOG2E))
        power_ref[head] = power
        weight_grad_ref[head] = weight_grad
        stats_ref[head, 0:1] = peak
        stats_ref[head, 1:2] = jnp.sum(power, axis=0, keepdims=True)
        stats_ref[head, 2:3] = jnp.sum(power * weight_grad, axis=0, keepdims=True)


def own_scores(pieces):
    tokens = len(pieces) * pieces[0].shape[1]
    heads = pieces[0].shape[-1] // HD
    square = jax.ShapeDtypeStruct((heads, tokens, tokens), F32)
    stats = jax.ShapeDtypeStruct((heads, 8, tokens), F32)
    return call(
        own_scores_body, [square, square, stats], [VM] * len(pieces), [VM] * 3, "own_scores", 16
    )(*pieces)


def near_scores_body(frame_count, parts, *refs):
    piece_refs, panel_refs, (power_ref, weight_grad_ref, stats_ref) = refs[:parts], refs[parts:-3], refs[-3:]
    hidden, spans = hidden_and_spans(frame_count, panel_refs, SWAPS[: len(panel_refs)])
    for head in range(piece_refs[0].shape[-1] // HD):
        query, grad = [rows_of(piece_refs, i, head) for i in (2, 3)]
        scores = dot(panel_rows(panel_refs, 0, head), query, (1, 1))
        weight_grad = dot(panel_rows(panel_refs, 1, head), grad, (1, 1))
        weight_grad_ref[head] = weight_grad
        peaks = [jnp.max(scores[span], axis=0, keepdims=True) + bias for span, bias in zip(spans, hidden)]
        peak = jnp.maximum(functools.reduce(jnp.maximum, peaks), LOWEST)
        total = moment = 0.0
        for span, bias in zip(spans, hidden):
            power = jnp.exp2((scores[span] - (peak - bias)) * (SCALE * LOG2E))
            power_ref[head, span] = power
            total = total + jnp.sum(power, axis=0, keepdims=True)
            moment = moment + jnp.sum(power * weight_grad[span], axis=0, keepdims=True)
        stats_ref[head, 0:1] = peak
        stats_ref[head, 1:2] = total
        stats_ref[head, 2:3] = moment


def near_scores(pieces, panels):
    parts = len(pieces)
    _, rows, width = pieces[0].shape
    tokens = parts * rows
    square = jax.ShapeDtypeStruct((width // HD, sum(p.shape[0] for p in panels) * rows, tokens), F32)
    stats = jax.ShapeDtypeStruct((width // HD, 8, tokens), F32)
    body = functools.partial(near_scores_body, lax.axis_size("frame"), parts)
    return call(
        body, [square, square, stats], [VM] * (parts + len(panels)), [VM] * 3, "near_scores", 16
    )(*pieces, *panels)


def hidden_and_spans(frame_count, panel_refs, swaps):
    frame = lax.axis_index("frame")
    hidden = [jnp.where(has_partner(frame, frame_count, *swap), 0.0, -jnp.inf).astype(F32) for swap in swaps]
    sizes = [ref.shape[0] * ref.shape[2] for ref in panel_refs]
    return hidden, [slice(sum(sizes[:i]), sum(sizes[: i + 1])) for i in range(len(sizes))]


def remote_part_body(frame_count, parts, *refs):
    piece_refs, far_refs, refs = refs[:parts], refs[parts : parts + 2], refs[parts + 2 :]
    stats_ref, near_stats_ref, power_ref, weight_grad_ref, joint_ref, *target_refs, low_ref, score_grad_ref = refs
    rows = piece_refs[0].shape[1]
    hidden, spans = hidden_and_spans(frame_count, far_refs, SWAPS[2:])
    near = power_ref.shape[1]
    for head in range(piece_refs[0].shape[-1] // HD):
        query, grad = [rows_of(piece_refs, i, head) for i in (2, 3)]
        scores = dot(panel_rows(far_refs, 0, head), query, (1, 1))
        weight_grad = dot(panel_rows(far_refs, 1, head), grad, (1, 1))
        parts_before = (stats_ref, near_stats_ref)
        peaks = [jnp.max(scores[span], axis=0, keepdims=True) + bias for span, bias in zip(spans, hidden)]
        peak = functools.reduce(jnp.maximum, peaks + [ref[head, 0:1] for ref in parts_before])
        rescales = [jnp.exp2((ref[head, 0:1] - peak) * (SCALE * LOG2E)) for ref in parts_before]
        powers = [
            jnp.exp2((scores[span] - (peak - bias)) * (SCALE * LOG2E)) for span, bias in zip(spans, hidden)
        ]
        totals = [jnp.sum(p, axis=0, keepdims=True) for p in powers]
        totals += [ref[head, 1:2] * by for ref, by in zip(parts_before, rescales)]
        moments = [jnp.sum(p * weight_grad[span], axis=0, keepdims=True) for p, span in zip(powers, spans)]
        moments += [ref[head, 2:3] * by for ref, by in zip(parts_before, rescales)]
        inverse = 1.0 / functools.reduce(jnp.add, totals)
        delta = functools.reduce(jnp.add, moments) * inverse
        joint_ref[head, 0:1] = rescales[0] * inverse
        joint_ref[head, 1:2] = delta
        near_weights = power_ref[head] * (rescales[1] * inverse)
        weights = [near_weights] + [p * inverse for p in powers]
        weight_grads = [weight_grad_ref[head]] + [weight_grad[span] for span in spans]
        low = jnp.concatenate([w.astype(BF16) for w in weights], axis=0)
        score_grad = jnp.concatenate(
            [(w * (g - delta)).astype(BF16) for w, g in zip(weights, weight_grads)], axis=0
        )
        low_ref[head] = low
        score_grad_ref[head] = score_grad
        key_part = (dot(score_grad, query, (1, 0)) * SCALE).astype(BF16)
        value_part = dot(low, grad, (1, 0)).astype(BF16)
        start = 0
        for target in target_refs:
            size = target.shape[0] * rows
            target[:, 0, :, columns(head)] = key_part[start : start + size].reshape(-1, rows, HD)
            target[:, 1, :, columns(head)] = value_part[start : start + size].reshape(-1, rows, HD)
            start += size


def remote_part(pieces, panels, stats, near_stats, near_power, near_weight_grad):
    parts = len(pieces)
    _, rows, width = pieces[0].shape
    shape = jax.ShapeDtypeStruct
    square = shape((width // HD, sum(p.shape[0] for p in panels) * rows, parts * rows), BF16)
    outs = [shape(stats.shape, F32)] + [shape(p.shape, BF16) for p in panels] + [square, square]
    body = functools.partial(remote_part_body, lax.axis_size("frame"), parts)
    outs = call(body, outs, [VM] * (parts + 6), [VM] * 7, "remote_part", 24)(
        *pieces, *panels[2:], stats, near_stats, near_power, near_weight_grad
    )
    return outs[0], outs[1:5], outs[5], outs[6]


def own_grads_body(parts, *refs):
    piece_refs, panel_refs, refs = refs[:parts], refs[parts : parts + 4], refs[parts + 4 :]
    power_ref, weight_grad_ref, joint_ref, low_ref, score_grad_ref, first_ref, own_ref = refs
    _, rows, width = piece_refs[0].shape
    for head in range(width // HD):
        cols = columns(head)
        key, value, query, grad = [rows_of(piece_refs, i, head) for i in range(4)]
        weights = power_ref[head] * joint_ref[head, 0:1]
        score_grad = (weights * (weight_grad_ref[head] - joint_ref[head, 1:2])).astype(BF16)
        low = weights.astype(BF16)
        own_ref[:, 0, :, cols] = (dot(score_grad, query, (1, 0)) * SCALE).reshape(parts, rows, HD)
        own_ref[:, 1, :, cols] = dot(low, grad, (1, 0)).reshape(parts, rows, HD)
        query_t = dot(
            jnp.concatenate([key, panel_rows(panel_refs, 0, head)], axis=0),
            jnp.concatenate([score_grad, score_grad_ref[head]], axis=0),
            (0, 0),
        )
        out_t = dot(
            jnp.concatenate([value, panel_rows(panel_refs, 1, head)], axis=0),
            jnp.concatenate([low, low_ref[head]], axis=0),
            (0, 0),
        )
        attended = out_t.T.astype(BF16)
        query_grad = (query_t * SCALE).T.astype(BF16)
        for slot in range(parts):
            first_ref[slot, 0, :, cols] = attended[slot * rows : (slot + 1) * rows]
            first_ref[slot, 1, :, cols] = query_grad[slot * rows : (slot + 1) * rows]


def own_grads(pieces, panels, power, weight_grad, joint, lows, score_grads):
    parts = len(pieces)
    _, rows, width = pieces[0].shape
    two = (parts, 2, rows, width)
    outs = [jax.ShapeDtypeStruct(two, BF16), jax.ShapeDtypeStruct(two, F32)]
    body = functools.partial(own_grads_body, parts)
    return call(body, outs, [VM] * (parts + 9), [VM] * 2, "own_grads", 16)(
        *pieces, *panels, power, weight_grad, joint, lows, score_grads
    )


def add_returned(block_order, first, own, returned):
    parts, _, rows, width = own.shape
    per = BLK // rows

    def body(order_ref, first_ref, own_ref, a1_ref, b1_ref, a2_ref, b2_ref, *refs):
        out_refs, sum_ref = refs[:parts], refs[parts]
        frame = lax.axis_index("frame")
        for k in range(parts):
            sum_ref[place_below(k)] = own_ref[k]
        for rank in range(2):
            start = order_ref[rank, frame] * per
            for i in range(per):
                at = rank * per + i
                term = a1_ref[at].astype(F32) + b1_ref[at].astype(F32)
                if rank == 0:
                    term = term + (a2_ref[i].astype(F32) + b2_ref[i].astype(F32))
                sum_ref[start + i] = sum_ref[start + i] + term
        for k in range(parts):
            out_refs[k][0:2] = sum_ref[place_below(k)].astype(BF16)
            out_refs[k][2:4] = first_ref[k]

    shape = jax.ShapeDtypeStruct((4, rows, width), BF16)
    scratch = [pltpu.VMEM(own.shape, F32)]
    return call(
        body, [shape] * parts, [SM] + [VM] * 6, [VM] * parts, "add_returned", 10, scratch
    )(block_order, first, own, *returned)


def local(query_rows, key_rows, value_rows, out_grad, block_order):
    parts = lax.axis_size("head")
    block_order = pltpu.with_memory_space_constraint(block_order.T, pltpu.HBM)
    arrived = head_shifts(pack((key_rows, value_rows, query_rows, out_grad), parts), 1)
    near, far = pick_blocks(block_order, arrived)
    panels = [swapped(far if swap[0] == 2 else near, *swap) for swap in SWAPS]
    power, weight_grad, stats = own_scores(arrived)
    near_power, near_weight_grad, near_stats = near_scores(arrived, panels[:2])
    joint, parts_of_others, lows, score_grads = remote_part(
        arrived, panels, stats, near_stats, near_power, near_weight_grad
    )
    returned = [swapped(part, *swap) for part, swap in zip(parts_of_others, SWAPS)]
    first, own = own_grads(arrived, panels, power, weight_grad, joint, lows, score_grads)
    leaving = add_returned(block_order, first, own, returned)
    key_grad, value_grad, attended, query_grad = unpack(head_shifts(leaving, -1))
    return (attended, query_grad, key_grad, value_grad)


def solution(mesh):
    rows = P(("frame", "head"), None)
    return jax.shard_map(
        local,
        mesh=mesh,
        in_specs=(rows, rows, rows, rows, P()),
        out_specs=(rows, rows, rows, rows),
        check_vma=False,
    )
```

```python
import functools
import math

import jax
import jax.numpy as jnp
from jax import lax
from jax.experimental import pallas as pl
from jax.experimental.pallas import tpu as pltpu
from jax.sharding import PartitionSpec as P

HD = 128
BLK = 128
BF16 = jnp.bfloat16
F32 = jnp.float32
SCALE = 1.0 / math.sqrt(HD)
LOG2E = 1.0 / math.log(2.0)
MIB = 1024 * 1024
SHIFTS = (0, 1, 7, 2, 6, 3, 5, 4)

VM = pl.BlockSpec(memory_space=pltpu.VMEM)
SM = pl.BlockSpec(memory_space=pltpu.SMEM)


def call(body, out_shape, in_specs, out_specs, name, mib, scratch_shapes=()):
    return pl.pallas_call(
        body,
        out_shape=out_shape,
        in_specs=in_specs,
        out_specs=out_specs,
        scratch_shapes=scratch_shapes,
        name=name,
        compiler_params=pltpu.CompilerParams(vmem_limit_bytes=mib * MIB),
    )


def swapped(array, distance, start):
    length = lax.axis_size("frame")
    pairs = []
    for first in range(start, length, 2 * distance):
        for low in range(first, min(first + distance, length - distance)):
            pairs += [(low, low + distance), (low + distance, low)]
    return lax.ppermute(array, "frame", pairs)


SWAPS = ((1, 0), (1, 1), (2, 0), (2, 2))


def has_partner(frame, length, distance, start):
    shifted = frame + (2 * distance - start)
    lower_half = lax.rem(shifted, 2 * distance) < distance
    partner = jnp.where(lower_half, frame + distance, frame - distance)
    return jnp.logical_and(jnp.logical_and(partner >= 0, partner < length), frame >= 0)


def head_shifts(pieces, sign):
    length = lax.axis_size("head")
    arrived = []
    for piece, by in zip(pieces, SHIFTS):
        if by:
            flat = piece.reshape(-1, piece.shape[-1])
            flat = lax.ppermute(flat, "head", [(i, (i + sign * by) % length) for i in range(length)])
            piece = flat.reshape(piece.shape)
        arrived.append(piece)
    return arrived


def place_above(slot):
    length = lax.axis_size("head")
    return lax.rem(lax.axis_index("head") + SHIFTS[slot], length)


def place_below(slot):
    length = lax.axis_size("head")
    return lax.rem(lax.axis_index("head") + (length - SHIFTS[slot]), length)


def columns_of(slot, piece):
    return pl.ds(pl.multiple_of(place_above(slot) * piece, piece), piece)


def pack(arrays, parts):
    rows, width = arrays[0].shape
    count = len(arrays)
    piece = width // parts

    def body(*refs):
        in_refs, out_refs, (held, sem) = refs[:count], refs[count:-2], refs[-2:]
        copies = [pltpu.make_async_copy(ref, held.at[i], sem.at[i]) for i, ref in enumerate(in_refs)]
        for copy in copies:
            copy.start()
        for i, copy in enumerate(copies):
            copy.wait()
            for k, out_ref in enumerate(out_refs):
                out_ref[i] = held[i, :, columns_of(k, piece)]

    shape = jax.ShapeDtypeStruct((count, rows, piece), arrays[0].dtype)
    anywhere = pl.BlockSpec(memory_space=pltpu.HBM)
    arrays = [pltpu.with_memory_space_constraint(array, pltpu.HBM) for array in arrays]
    scratch = [pltpu.VMEM((count, rows, width), arrays[0].dtype), pltpu.SemaphoreType.DMA((count,))]
    return call(body, [shape] * parts, [anywhere] * count, [VM] * parts, "pack", 4, scratch)(*arrays)


def unpack(pieces):
    parts = len(pieces)
    count, rows, piece = pieces[0].shape

    def body(*refs):
        for i, ref in enumerate(refs[parts:]):
            for k in range(parts):
                ref[:, columns_of(k, piece)] = refs[k][i]

    shape = jax.ShapeDtypeStruct((rows, parts * piece), pieces[0].dtype)
    return call(body, [shape] * count, [VM] * parts, [VM] * count, "unpack", 8)(*pieces)


def pick_blocks(block_order, pieces):
    parts = len(pieces)
    _, rows, width = pieces[0].shape
    per = BLK // rows

    def body(order_ref, *refs):
        near_ref, far_ref, all_ref = refs[parts:]
        frame = lax.axis_index("frame")
        for k in range(parts):
            all_ref[place_below(k)] = refs[k][0:2]
        for rank in range(2):
            start = order_ref[rank, frame] * per
            for i in range(per):
                taken = all_ref[start + i]
                near_ref[rank * per + i] = taken
                if rank == 0:
                    far_ref[i] = taken

    near = jax.ShapeDtypeStruct((2 * per, 2, rows, width), BF16)
    far = jax.ShapeDtypeStruct((per, 2, rows, width), BF16)
    scratch = [pltpu.VMEM((parts, 2, rows, width), BF16)]
    return call(
        body, [near, far], [SM] + [VM] * parts, [VM, VM], "pick_blocks", 8, scratch
    )(block_order, *pieces)


def dot(a, b, contract):
    return lax.dot_general(a, b, ((contract[:1], contract[1:]), ((), ())), preferred_element_type=F32)


def columns(head):
    return slice(head * HD, (head + 1) * HD)


def rows_of(refs, i, head):
    return jnp.concatenate([ref[i, :, columns(head)] for ref in refs], axis=0)


def own_scores_body(*refs):
    piece_refs, (power_ref, weight_grad_ref, stats_ref) = refs[:-3], refs[-3:]
    for head in range(piece_refs[0].shape[-1] // HD):
        key, value, query, grad = [rows_of(piece_refs, i, head) for i in range(4)]
        scores = dot(key, query, (1, 1)) * (SCALE * LOG2E)
        weight_grad = dot(value, grad, (1, 1))
        peak = jnp.max(scores, axis=0, keepdims=True)
        power = jnp.exp2(scores - peak)
        power_ref[head] = power
        weight_grad_ref[head] = weight_grad
        stats_ref[head, 0:1] = peak
        stats_ref[head, 1:2] = jnp.sum(power, axis=0, keepdims=True)
        stats_ref[head, 2:3] = jnp.sum(power * weight_grad, axis=0, keepdims=True)


def own_scores(pieces):
    tokens = len(pieces) * pieces[0].shape[1]
    heads = pieces[0].shape[-1] // HD
    square = jax.ShapeDtypeStruct((heads, tokens, tokens), F32)
    stats = jax.ShapeDtypeStruct((heads, 8, tokens), F32)
    return call(
        own_scores_body, [square, square, stats], [VM] * len(pieces), [VM] * 3, "own_scores", 16
    )(*pieces)


def remote_part_body(frame_count, parts, *refs):
    piece_refs, panel_refs, stats_ref = refs[:parts], refs[parts : parts + 4], refs[parts + 4]
    joint_ref, *rest = refs[parts + 5 :]
    target_refs, low_refs, score_grad_refs = rest[:4], rest[4:8], rest[8:]
    frame = lax.axis_index("frame")
    rows = piece_refs[0].shape[1]
    heads = range(piece_refs[0].shape[-1] // HD)
    hidden = [
        jnp.where(has_partner(frame, frame_count, *swap), 0.0, -jnp.inf).astype(F32) for swap in SWAPS
    ]
    queries = [rows_of(piece_refs, 2, head) for head in heads]
    grads = [rows_of(piece_refs, 3, head) for head in heads]
    scores = [
        [
            dot(ref[:, 0, :, columns(head)].reshape(-1, HD), queries[head], (1, 1)) * (SCALE * LOG2E) + bias
            for ref, bias in zip(panel_refs, hidden)
        ]
        for head in heads
    ]
    weight_grads = [
        [dot(ref[:, 1, :, columns(head)].reshape(-1, HD), grads[head], (1, 1)) for ref in panel_refs]
        for head in heads
    ]
    for head in heads:
        own_peak = stats_ref[head, 0:1]
        peaks = [jnp.max(s, axis=0, keepdims=True) for s in scores[head]]
        peak = functools.reduce(jnp.maximum, peaks, own_peak)
        powers = [jnp.exp2(s - peak) for s in scores[head]]
        rescale = jnp.exp2(own_peak - peak)
        total = functools.reduce(
            jnp.add, [jnp.sum(p, axis=0, keepdims=True) for p in powers], stats_ref[head, 1:2] * rescale
        )
        moment = functools.reduce(
            jnp.add,
            [jnp.sum(p * g, axis=0, keepdims=True) for p, g in zip(powers, weight_grads[head])],
            stats_ref[head, 2:3] * rescale,
        )
        inverse = 1.0 / total
        delta = moment * inverse
        joint_ref[head, 0:1] = rescale * inverse
        joint_ref[head, 1:2] = delta
        for power, weight_grad, low_ref, score_grad_ref in zip(
            powers, weight_grads[head], low_refs, score_grad_refs
        ):
            weights = power * inverse
            low_ref[head] = weights.astype(BF16)
            score_grad_ref[head] = (weights * (weight_grad - delta)).astype(BF16)
    for head in heads:
        cols = columns(head)
        for target, low_ref, score_grad_ref in zip(target_refs, low_refs, score_grad_refs):
            key_part = dot(score_grad_ref[head], queries[head], (1, 0)) * SCALE
            value_part = dot(low_ref[head], grads[head], (1, 0))
            target[:, 0, :, cols] = key_part.astype(BF16).reshape(-1, rows, HD)
            target[:, 1, :, cols] = value_part.astype(BF16).reshape(-1, rows, HD)


def remote_part(pieces, panels, stats):
    parts = len(pieces)
    _, rows, width = pieces[0].shape
    shape = jax.ShapeDtypeStruct
    squares = [shape((width // HD, p.shape[0] * rows, parts * rows), BF16) for p in panels]
    outs = [shape(stats.shape, F32)] + [shape(p.shape, BF16) for p in panels] + squares + squares
    body = functools.partial(remote_part_body, lax.axis_size("frame"), parts)
    outs = call(body, outs, [VM] * (parts + 5), [VM] * 13, "remote_part", 24)(*pieces, *panels, stats)
    return outs[0], outs[1:5], outs[5:9], outs[9:]


def own_grads_body(parts, *refs):
    piece_refs, panel_refs, refs = refs[:parts], refs[parts : parts + 4], refs[parts + 4 :]
    power_ref, weight_grad_ref, joint_ref = refs[:3]
    low_refs, score_grad_refs, (first_ref, own_ref) = refs[3:7], refs[7:11], refs[11:]
    _, rows, width = piece_refs[0].shape
    for head in range(width // HD):
        cols = columns(head)
        key, value, query, grad = [rows_of(piece_refs, i, head) for i in range(4)]
        weights = power_ref[head] * joint_ref[head, 0:1]
        score_grad = (weights * (weight_grad_ref[head] - joint_ref[head, 1:2])).astype(BF16)
        low = weights.astype(BF16)
        own_ref[:, 0, :, cols] = (dot(score_grad, query, (1, 0)) * SCALE).reshape(parts, rows, HD)
        own_ref[:, 1, :, cols] = dot(low, grad, (1, 0)).reshape(parts, rows, HD)
        query_t = dot(key, score_grad, (0, 0))
        out_t = dot(value, low, (0, 0))
        for panel_ref, low_ref, score_grad_ref in zip(panel_refs, low_refs, score_grad_refs):
            query_t = query_t + dot(panel_ref[:, 0, :, cols].reshape(-1, HD), score_grad_ref[head], (0, 0))
            out_t = out_t + dot(panel_ref[:, 1, :, cols].reshape(-1, HD), low_ref[head], (0, 0))
        attended = out_t.T.astype(BF16)
        query_grad = (query_t * SCALE).T.astype(BF16)
        for slot in range(parts):
            first_ref[slot, 0, :, cols] = attended[slot * rows : (slot + 1) * rows]
            first_ref[slot, 1, :, cols] = query_grad[slot * rows : (slot + 1) * rows]


def own_grads(pieces, panels, power, weight_grad, joint, lows, score_grads):
    parts = len(pieces)
    _, rows, width = pieces[0].shape
    two = (parts, 2, rows, width)
    outs = [jax.ShapeDtypeStruct(two, BF16), jax.ShapeDtypeStruct(two, F32)]
    body = functools.partial(own_grads_body, parts)
    return call(body, outs, [VM] * (parts + 15), [VM] * 2, "own_grads", 16)(
        *pieces, *panels, power, weight_grad, joint, *lows, *score_grads
    )


def add_returned(block_order, first, own, returned):
    parts, _, rows, width = own.shape
    per = BLK // rows

    def body(order_ref, first_ref, own_ref, a1_ref, b1_ref, a2_ref, b2_ref, *refs):
        out_refs, sum_ref = refs[:parts], refs[parts]
        frame = lax.axis_index("frame")
        for k in range(parts):
            sum_ref[place_below(k)] = own_ref[k]
        for rank in range(2):
            start = order_ref[rank, frame] * per
            for i in range(per):
                at = rank * per + i
                term = a1_ref[at].astype(F32) + b1_ref[at].astype(F32)
                if rank == 0:
                    term = term + (a2_ref[i].astype(F32) + b2_ref[i].astype(F32))
                sum_ref[start + i] = sum_ref[start + i] + term
        for k in range(parts):
            out_refs[k][0:2] = sum_ref[place_below(k)].astype(BF16)
            out_refs[k][2:4] = first_ref[k]

    shape = jax.ShapeDtypeStruct((4, rows, width), BF16)
    scratch = [pltpu.VMEM(own.shape, F32)]
    return call(
        body, [shape] * parts, [SM] + [VM] * 6, [VM] * parts, "add_returned", 10, scratch
    )(block_order, first, own, *returned)


def local(query_rows, key_rows, value_rows, out_grad, block_order):
    parts = lax.axis_size("head")
    block_order = pltpu.with_memory_space_constraint(block_order.T, pltpu.HBM)
    arrived = head_shifts(pack((key_rows, value_rows, query_rows, out_grad), parts), 1)
    near, far = pick_blocks(block_order, arrived)
    panels = [swapped(far if swap[0] == 2 else near, *swap) for swap in SWAPS]
    power, weight_grad, stats = own_scores(arrived)
    joint, parts_of_others, lows, score_grads = remote_part(arrived, panels, stats)
    returned = [swapped(part, *swap) for part, swap in zip(parts_of_others, SWAPS)]
    first, own = own_grads(arrived, panels, power, weight_grad, joint, lows, score_grads)
    leaving = add_returned(block_order, first, own, returned)
    key_grad, value_grad, attended, query_grad = unpack(head_shifts(leaving, -1))
    return (attended, query_grad, key_grad, value_grad)


def solution(mesh):
    rows = P(("frame", "head"), None)
    return jax.shard_map(
        local,
        mesh=mesh,
        in_specs=(rows, rows, rows, rows, P()),
        out_specs=(rows, rows, rows, rows),
        check_vma=False,
    )
```

```python
import functools
import math

import jax
import jax.numpy as jnp
from jax import lax
from jax.experimental import pallas as pl
from jax.experimental.pallas import tpu as pltpu
from jax.sharding import PartitionSpec as P

HD = 128
BLK = 128
BF16 = jnp.bfloat16
F32 = jnp.float32
SCALE = 1.0 / math.sqrt(HD)
LOG2E = 1.0 / math.log(2.0)
MIB = 1024 * 1024
SHIFTS = (0, 1, 7, 2, 6, 3, 5, 4)

LOWEST = -1e30

VM = pl.BlockSpec(memory_space=pltpu.VMEM)
SM = pl.BlockSpec(memory_space=pltpu.SMEM)


def call(body, out_shape, in_specs, out_specs, name, mib, scratch_shapes=()):
    return pl.pallas_call(
        body,
        out_shape=out_shape,
        in_specs=in_specs,
        out_specs=out_specs,
        scratch_shapes=scratch_shapes,
        name=name,
        compiler_params=pltpu.CompilerParams(vmem_limit_bytes=mib * MIB),
    )


def swapped(array, distance, start):
    length = lax.axis_size("frame")
    pairs = []
    for first in range(start, length, 2 * distance):
        for low in range(first, min(first + distance, length - distance)):
            pairs += [(low, low + distance), (low + distance, low)]
    return lax.ppermute(array, "frame", pairs)


SWAPS = ((1, 0), (1, 1), (2, 0), (2, 2))


def has_partner(frame, length, distance, start):
    shifted = frame + (2 * distance - start)
    lower_half = lax.rem(shifted, 2 * distance) < distance
    partner = jnp.where(lower_half, frame + distance, frame - distance)
    return jnp.logical_and(jnp.logical_and(partner >= 0, partner < length), frame >= 0)


def head_shifts(pieces, sign):
    length = lax.axis_size("head")
    arrived = []
    for piece, by in zip(pieces, SHIFTS):
        if by:
            flat = piece.reshape(-1, piece.shape[-1])
            flat = lax.ppermute(flat, "head", [(i, (i + sign * by) % length) for i in range(length)])
            piece = flat.reshape(piece.shape)
        arrived.append(piece)
    return arrived


def place_above(slot):
    length = lax.axis_size("head")
    return lax.rem(lax.axis_index("head") + SHIFTS[slot], length)


def place_below(slot):
    length = lax.axis_size("head")
    return lax.rem(lax.axis_index("head") + (length - SHIFTS[slot]), length)


def columns_of(slot, piece):
    return pl.ds(pl.multiple_of(place_above(slot) * piece, piece), piece)


def pack(arrays, parts):
    rows, width = arrays[0].shape
    count = len(arrays)
    piece = width // parts

    def body(*refs):
        in_refs, out_refs, (held, sem) = refs[:count], refs[count:-2], refs[-2:]
        copies = [pltpu.make_async_copy(ref, held.at[i], sem.at[i]) for i, ref in enumerate(in_refs)]
        for copy in copies:
            copy.start()
        for i, copy in enumerate(copies):
            copy.wait()
            for k, out_ref in enumerate(out_refs):
                out_ref[i] = held[i, :, columns_of(k, piece)]

    shape = jax.ShapeDtypeStruct((count, rows, piece), arrays[0].dtype)
    anywhere = pl.BlockSpec(memory_space=pltpu.HBM)
    arrays = [pltpu.with_memory_space_constraint(array, pltpu.HBM) for array in arrays]
    scratch = [pltpu.VMEM((count, rows, width), arrays[0].dtype), pltpu.SemaphoreType.DMA((count,))]
    return call(body, [shape] * parts, [anywhere] * count, [VM] * parts, "pack", 4, scratch)(*arrays)


def unpack(pieces):
    parts = len(pieces)
    count, rows, piece = pieces[0].shape

    def body(*refs):
        for i, ref in enumerate(refs[parts:]):
            for k in range(parts):
                ref[:, columns_of(k, piece)] = refs[k][i]

    shape = jax.ShapeDtypeStruct((rows, parts * piece), pieces[0].dtype)
    return call(body, [shape] * count, [VM] * parts, [VM] * count, "unpack", 8)(*pieces)


def pick_blocks(block_order, pieces):
    parts = len(pieces)
    _, rows, width = pieces[0].shape
    per = BLK // rows

    def body(order_ref, *refs):
        near_ref, far_ref, all_ref = refs[parts:]
        frame = lax.axis_index("frame")
        for k in range(parts):
            all_ref[place_below(k)] = refs[k][0:2]
        for rank in range(2):
            start = order_ref[rank, frame] * per
            for i in range(per):
                taken = all_ref[start + i]
                near_ref[rank * per + i] = taken
                if rank == 0:
                    far_ref[i] = taken

    near = jax.ShapeDtypeStruct((2 * per, 2, rows, width), BF16)
    far = jax.ShapeDtypeStruct((per, 2, rows, width), BF16)
    scratch = [pltpu.VMEM((parts, 2, rows, width), BF16)]
    return call(
        body, [near, far], [SM] + [VM] * parts, [VM, VM], "pick_blocks", 8, scratch
    )(block_order, *pieces)


def dot(a, b, contract):
    return lax.dot_general(a, b, ((contract[:1], contract[1:]), ((), ())), preferred_element_type=F32)


def columns(head):
    return slice(head * HD, (head + 1) * HD)


def rows_of(refs, i, head):
    return jnp.concatenate([ref[i, :, columns(head)] for ref in refs], axis=0)


def panel_rows(refs, i, head):
    return jnp.concatenate([ref[:, i, :, columns(head)].reshape(-1, HD) for ref in refs], axis=0)


def own_scores_body(*refs):
    piece_refs, (power_ref, weight_grad_ref, stats_ref) = refs[:-3], refs[-3:]
    for head in range(piece_refs[0].shape[-1] // HD):
        key, value, query, grad = [rows_of(piece_refs, i, head) for i in range(4)]
        scores = dot(key, query, (1, 1))
        weight_grad = dot(value, grad, (1, 1))
        peak = jnp.max(scores, axis=0, keepdims=True)
        power = jnp.exp2((scores - peak) * (SCALE * LOG2E))
        power_ref[head] = power
        weight_grad_ref[head] = weight_grad
        stats_ref[head, 0:1] = peak
        stats_ref[head, 1:2] = jnp.sum(power, axis=0, keepdims=True)
        stats_ref[head, 2:3] = jnp.sum(power * weight_grad, axis=0, keepdims=True)


def own_scores(pieces):
    tokens = len(pieces) * pieces[0].shape[1]
    heads = pieces[0].shape[-1] // HD
    square = jax.ShapeDtypeStruct((heads, tokens, tokens), F32)
    stats = jax.ShapeDtypeStruct((heads, 8, tokens), F32)
    return call(
        own_scores_body, [square, square, stats], [VM] * len(pieces), [VM] * 3, "own_scores", 16
    )(*pieces)


def near_scores_body(frame_count, parts, *refs):
    piece_refs, panel_refs, (power_ref, weight_grad_ref, stats_ref) = refs[:parts], refs[parts:-3], refs[-3:]
    hidden, spans = hidden_and_spans(frame_count, panel_refs, SWAPS[: len(panel_refs)])
    for head in range(piece_refs[0].shape[-1] // HD):
        query, grad = [rows_of(piece_refs, i, head) for i in (2, 3)]
        scores = dot(panel_rows(panel_refs, 0, head), query, (1, 1))
        weight_grad = dot(panel_rows(panel_refs, 1, head), grad, (1, 1))
        weight_grad_ref[head] = weight_grad
        peaks = [jnp.max(scores[span], axis=0, keepdims=True) + bias for span, bias in zip(spans, hidden)]
        peak = jnp.maximum(functools.reduce(jnp.maximum, peaks), LOWEST)
        total = moment = 0.0
        for span, bias in zip(spans, hidden):
            power = jnp.exp2((scores[span] - (peak - bias)) * (SCALE * LOG2E))
            power_ref[head, span] = power
            total = total + jnp.sum(power, axis=0, keepdims=True)
            moment = moment + jnp.sum(power * weight_grad[span], axis=0, keepdims=True)
        stats_ref[head, 0:1] = peak
        stats_ref[head, 1:2] = total
        stats_ref[head, 2:3] = moment


def near_scores(pieces, panels):
    parts = len(pieces)
    _, rows, width = pieces[0].shape
    tokens = parts * rows
    square = jax.ShapeDtypeStruct((width // HD, sum(p.shape[0] for p in panels) * rows, tokens), F32)
    stats = jax.ShapeDtypeStruct((width // HD, 8, tokens), F32)
    body = functools.partial(near_scores_body, lax.axis_size("frame"), parts)
    return call(
        body, [square, square, stats], [VM] * (parts + len(panels)), [VM] * 3, "near_scores", 16
    )(*pieces, *panels)


def hidden_and_spans(frame_count, panel_refs, swaps):
    frame = lax.axis_index("frame")
    hidden = [jnp.where(has_partner(frame, frame_count, *swap), 0.0, -jnp.inf).astype(F32) for swap in swaps]
    sizes = [ref.shape[0] * ref.shape[2] for ref in panel_refs]
    return hidden, [slice(sum(sizes[:i]), sum(sizes[: i + 1])) for i in range(len(sizes))]


def remote_part_body(frame_count, parts, *refs):
    piece_refs, far_refs, refs = refs[:parts], refs[parts : parts + 2], refs[parts + 2 :]
    stats_ref, near_stats_ref, power_ref, weight_grad_ref, joint_ref, *target_refs, low_ref, score_grad_ref = refs
    rows = piece_refs[0].shape[1]
    hidden, spans = hidden_and_spans(frame_count, far_refs, SWAPS[2:])
    near = power_ref.shape[1]
    for head in range(piece_refs[0].shape[-1] // HD):
        query, grad = [rows_of(piece_refs, i, head) for i in (2, 3)]
        scores = dot(panel_rows(far_refs, 0, head), query, (1, 1))
        weight_grad = dot(panel_rows(far_refs, 1, head), grad, (1, 1))
        parts_before = (stats_ref, near_stats_ref)
        peaks = [jnp.max(scores[span], axis=0, keepdims=True) + bias for span, bias in zip(spans, hidden)]
        peak = functools.reduce(jnp.maximum, peaks + [ref[head, 0:1] for ref in parts_before])
        rescales = [jnp.exp2((ref[head, 0:1] - peak) * (SCALE * LOG2E)) for ref in parts_before]
        powers = [
            jnp.exp2((scores[span] - (peak - bias)) * (SCALE * LOG2E)) for span, bias in zip(spans, hidden)
        ]
        totals = [jnp.sum(p, axis=0, keepdims=True) for p in powers]
        totals += [ref[head, 1:2] * by for ref, by in zip(parts_before, rescales)]
        moments = [jnp.sum(p * weight_grad[span], axis=0, keepdims=True) for p, span in zip(powers, spans)]
        moments += [ref[head, 2:3] * by for ref, by in zip(parts_before, rescales)]
        inverse = 1.0 / functools.reduce(jnp.add, totals)
        delta = functools.reduce(jnp.add, moments) * inverse
        joint_ref[head, 0:1] = rescales[0] * inverse
        joint_ref[head, 1:2] = delta
        near_weights = power_ref[head] * (rescales[1] * inverse)
        weights = [near_weights] + [p * inverse for p in powers]
        weight_grads = [weight_grad_ref[head]] + [weight_grad[span] for span in spans]
        low = jnp.concatenate([w.astype(BF16) for w in weights], axis=0)
        score_grad = jnp.concatenate(
            [(w * (g - delta)).astype(BF16) for w, g in zip(weights, weight_grads)], axis=0
        )
        low_ref[head] = low
        score_grad_ref[head] = score_grad
        key_part = (dot(score_grad, query, (1, 0)) * SCALE).astype(BF16)
        value_part = dot(low, grad, (1, 0)).astype(BF16)
        start = 0
        for target in target_refs:
            size = target.shape[0] * rows
            target[:, 0, :, columns(head)] = key_part[start : start + size].reshape(-1, rows, HD)
            target[:, 1, :, columns(head)] = value_part[start : start + size].reshape(-1, rows, HD)
            start += size


def remote_part(pieces, panels, stats, near_stats, near_power, near_weight_grad):
    parts = len(pieces)
    _, rows, width = pieces[0].shape
    shape = jax.ShapeDtypeStruct
    square = shape((width // HD, sum(p.shape[0] for p in panels) * rows, parts * rows), BF16)
    outs = [shape(stats.shape, F32)] + [shape(p.shape, BF16) for p in panels] + [square, square]
    body = functools.partial(remote_part_body, lax.axis_size("frame"), parts)
    outs = call(body, outs, [VM] * (parts + 6), [VM] * 7, "remote_part", 24)(
        *pieces, *panels[2:], stats, near_stats, near_power, near_weight_grad
    )
    return outs[0], outs[1:5], outs[5], outs[6]


def own_grads_body(parts, *refs):
    piece_refs, panel_refs, refs = refs[:parts], refs[parts : parts + 4], refs[parts + 4 :]
    power_ref, weight_grad_ref, joint_ref, low_ref, score_grad_ref, first_ref, own_ref = refs
    _, rows, width = piece_refs[0].shape
    for head in range(width // HD):
        cols = columns(head)
        key, value, query, grad = [rows_of(piece_refs, i, head) for i in range(4)]
        weights = power_ref[head] * joint_ref[head, 0:1]
        score_grad = (weights * (weight_grad_ref[head] - joint_ref[head, 1:2])).astype(BF16)
        low = weights.astype(BF16)
        own_ref[:, 0, :, cols] = (dot(score_grad, query, (1, 0)) * SCALE).reshape(parts, rows, HD)
        own_ref[:, 1, :, cols] = dot(low, grad, (1, 0)).reshape(parts, rows, HD)
        query_t = dot(
            jnp.concatenate([key, panel_rows(panel_refs, 0, head)], axis=0),
            jnp.concatenate([score_grad, score_grad_ref[head]], axis=0),
            (0, 0),
        )
        out_t = dot(
            jnp.concatenate([value, panel_rows(panel_refs, 1, head)], axis=0),
            jnp.concatenate([low, low_ref[head]], axis=0),
            (0, 0),
        )
        attended = out_t.T.astype(BF16)
        query_grad = (query_t * SCALE).T.astype(BF16)
        for slot in range(parts):
            first_ref[slot, 0, :, cols] = attended[slot * rows : (slot + 1) * rows]
            first_ref[slot, 1, :, cols] = query_grad[slot * rows : (slot + 1) * rows]


def own_grads(pieces, panels, power, weight_grad, joint, lows, score_grads):
    parts = len(pieces)
    _, rows, width = pieces[0].shape
    two = (parts, 2, rows, width)
    outs = [jax.ShapeDtypeStruct(two, BF16), jax.ShapeDtypeStruct(two, F32)]
    body = functools.partial(own_grads_body, parts)
    return call(body, outs, [VM] * (parts + 9), [VM] * 2, "own_grads", 16)(
        *pieces, *panels, power, weight_grad, joint, lows, score_grads
    )


def add_returned(block_order, first, own, returned):
    parts, _, rows, width = own.shape
    per = BLK // rows

    def body(order_ref, first_ref, own_ref, a1_ref, b1_ref, a2_ref, b2_ref, *refs):
        out_refs, sum_ref = refs[:parts], refs[parts]
        frame = lax.axis_index("frame")
        for k in range(parts):
            sum_ref[place_below(k)] = own_ref[k]
        for rank in range(2):
            start = order_ref[rank, frame] * per
            for i in range(per):
                at = rank * per + i
                term = a1_ref[at].astype(F32) + b1_ref[at].astype(F32)
                if rank == 0:
                    term = term + (a2_ref[i].astype(F32) + b2_ref[i].astype(F32))
                sum_ref[start + i] = sum_ref[start + i] + term
        for k in range(parts):
            out_refs[k][0:2] = sum_ref[place_below(k)].astype(BF16)
            out_refs[k][2:4] = first_ref[k]

    shape = jax.ShapeDtypeStruct((4, rows, width), BF16)
    scratch = [pltpu.VMEM(own.shape, F32)]
    return call(
        body, [shape] * parts, [SM] + [VM] * 6, [VM] * parts, "add_returned", 10, scratch
    )(block_order, first, own, *returned)


def local(query_rows, key_rows, value_rows, out_grad, block_order):
    parts = lax.axis_size("head")
    block_order = pltpu.with_memory_space_constraint(block_order.T, pltpu.HBM)
    arrived = head_shifts(pack((key_rows, value_rows, query_rows, out_grad), parts), 1)
    near, far = pick_blocks(block_order, arrived)
    panels = [swapped(far if swap[0] == 2 else near, *swap) for swap in SWAPS]
    power, weight_grad, stats = own_scores(arrived)
    near_power, near_weight_grad, near_stats = near_scores(arrived, panels[:2])
    joint, parts_of_others, lows, score_grads = remote_part(
        arrived, panels, stats, near_stats, near_power, near_weight_grad
    )
    returned = [swapped(part, *swap) for part, swap in zip(parts_of_others, SWAPS)]
    first, own = own_grads(arrived, panels, power, weight_grad, joint, lows, score_grads)
    leaving = add_returned(block_order, first, own, returned)
    key_grad, value_grad, attended, query_grad = unpack(head_shifts(leaving, -1))
    return (attended, query_grad, key_grad, value_grad)


def solution(mesh):
    rows = P(("frame", "head"), None)
    return jax.shard_map(
        local,
        mesh=mesh,
        in_specs=(rows, rows, rows, rows, P()),
        out_specs=(rows, rows, rows, rows),
        check_vma=False,
    )
```
